32 devices in a mesh: dp: 8 (over z, core), tensor: 4 (over y, x).
Axes of the slice: x: 2, y: 2, z: 4, core: 2. Of those that a mesh axis runs over, the one named last changes fastest.
Arguments:
- tokens: bfloat16 [8192, 1536], P(('dp', 'tensor')), may hold values from -6 to 6
- segments: int32 [8, 1024], P('dp'), may hold values from 0 to 3, never falling along the last dimension, each value on 1 to 512 neighbouring positions
- gains: float32 [2, 2, 1536], replicated, may hold values from 0.1 to 1.9
- q_weight: bfloat16 [2, 1536, 1536], P(None, 'dp', 'tensor'), as said below
- key_matrix: bfloat16 [2, 1536, 768], P(None, 'dp', 'tensor'), as said below
- value_matrix: bfloat16 [2, 1536, 768], P(None, 'dp', 'tensor'), may hold values from -0.15625 to 0.15625
- o_weight: bfloat16 [2, 1536, 1536], P(None, 'tensor', 'dp'), may hold values from -0.625 to 0.625
- gate_weight: bfloat16 [2, 1536, 4096], P(None, 'dp', 'tensor'), may hold values from -0.15625 to 0.15625
- up_weight: bfloat16 [2, 1536, 4096], P(None, 'dp', 'tensor'), may hold values from -0.15625 to 0.15625
- down_weight: bfloat16 [2, 4096, 1536], P(None, 'tensor', 'dp'), may hold values from -0.09375 to 0.09375
- cotangent: bfloat16 [8192, 1536], P(('dp', 'tensor')), may hold values from -6 to 6
Outputs:
- result: bfloat16 [8192, 1536], P(('dp', 'tensor'))
- input_grad: float32 [8192, 1536], P(('dp', 'tensor'))
- gains_grad: float32 [2, 2, 1536], P(None, None, ('dp', 'tensor'))
- q_weight_grad: float32 [2, 1536, 1536], P(None, 'dp', 'tensor')
- k_weight_grad: float32 [2, 1536, 768], P(None, 'dp', 'tensor')
- v_weight_grad: float32 [2, 1536, 768], P(None, 'dp', 'tensor')
- o_weight_grad: float32 [2, 1536, 1536], P(None, 'tensor', 'dp')
- gate_weight_grad: float32 [2, 1536, 4096], P(None, 'dp', 'tensor')
- up_weight_grad: float32 [2, 1536, 4096], P(None, 'dp', 'tensor')
- down_weight_grad: float32 [2, 4096, 1536], P(None, 'tensor', 'dp')
The draws below stay inside these ranges and needn't reach their ends.
Inputs may be any that keep to these rules, and one draw needn't show every extreme that they name: `segments`: in each row the document numbers never fall; every number appears, each in a run of at most 512 tokens, and some run has exactly 512. `q_weight`: real-valued entries of order 1536 ** -0.5 or a few times that. `key_matrix`: real-valued entries of order 1536 ** -0.5 or a few times that.
All inputs are finite; a program needn't handle non-finite values.
Results may differ from the reference program's by a relative error of at most 0.025.
The reference program's roundings to bfloat16 on the way count: a program that leaves them out, or rounds other values in their place, can miss the bound.
Values may be sent and summed in bfloat16 or wider, within the bound.
No kernel may reach another device: no remote copies, remote signals or barrier semaphores. Data moves between devices by JAX's collectives and lax.ppermute only.
A program may use at most 256 MiB of HBM per device.

```python
import math
import jax
import jax.numpy as jnp
import numpy as np
from jax import lax

MODEL_WIDTH = 1536
QUERY_HEADS = 16
KEY_VALUE_HEADS = 8
HEAD_SIZE = 96
FF = 4096
LEN = 1024
DECODER_LAYERS = 2
SEQS = 8
TOKENS = 8192


def common_query(key):
    base_draw = jax.random.normal(jax.random.fold_in(key, 11), (DECODER_LAYERS, MODEL_WIDTH, QUERY_HEADS * HEAD_SIZE), jnp.float32)
    return jnp.clip(base_draw, -6.0, 6.0) / math.sqrt(MODEL_WIDTH)


def draw_q_weight(key, part):
    base_draw = common_query(key)
    return base_draw.astype(jnp.bfloat16)


def draw_key_matrix(key, part):
    private_sample = jnp.clip(jax.random.normal(jax.random.fold_in(key, 13), (DECODER_LAYERS, MODEL_WIDTH, KEY_VALUE_HEADS * HEAD_SIZE), jnp.float32), -6.0, 6.0) / math.sqrt(MODEL_WIDTH)
    return private_sample.astype(jnp.bfloat16)


def steps_of(own_key, extent, cuts, least, high):
    def one(axis_at, blocks):
        steps = jax.random.uniform(jax.random.fold_in(jax.random.fold_in(own_key, 6), axis_at), (blocks,), jnp.float32, least / len(cuts), high / len(cuts))
        return jnp.repeat(jnp.exp(steps), extent[axis_at] // blocks).reshape((-1,) + (1,) * (len(extent) - axis_at - 1))

    factor_of = one(*cuts[0])
    for cut in cuts[1:]:
        factor_of = factor_of * one(*cut)
    return factor_of


def profile(count, total, limit, lean):
    portions = [(1 << 20) // math.isqrt(standing ** lean) + 1 for standing in range(2, count + 1)]
    spare, given = total - limit - (count - 1), [1] * (count - 1)
    while spare > 0:
        movable = [i for i in range(count - 1) if given[i] < limit]
        pool, budget = sum([portions[i] for i in movable]), spare
        for i in movable:
            extra = min(limit - given[i], max(1, budget * portions[i] // pool), spare)
            given[i] = given[i] + extra
            spare = spare - extra
    return np.array([limit] + given)


def uneven(key, count, total, reach, slope):
    if count == 2:
        one = jax.random.randint(key, (), max(1, total - reach), min(reach, total - 1) + 1)
        return jnp.stack([one, total - one])
    tallies = jnp.asarray(profile(count, total, reach, slope), jnp.int32)
    pairs = (count - 1) // 2
    giver, taker = tallies[1:1 + 2 * pairs:2], tallies[2:2 + 2 * pairs:2]
    margin = jnp.minimum(giver - 1, reach - taker)
    moved = jax.random.randint(jax.random.fold_in(key, 1), (pairs,), 0, 1 << 20) % (margin + 1)
    tallies = tallies.at[1:1 + 2 * pairs:2].set(giver - moved).at[2:2 + 2 * pairs:2].set(taker + moved)
    return tallies[jax.random.permutation(jax.random.fold_in(key, 2), count)]


def centred(rng, dims, spread, reach, cuts=(), held_as=jnp.bfloat16):
    factor_of = steps_of(rng, dims, cuts, -0.22, 0.18) if cuts else 1.0
    values = jax.random.normal(rng, dims, jnp.float32) * spread * factor_of
    return jnp.minimum(jnp.maximum(values, -reach), reach).astype(held_as)


def setup_inputs(seed: int = 0) -> dict:
    arg_keys = jax.random.split(jax.random.key(seed), 12)
    return {
        "tokens": centred(arg_keys[0], (TOKENS, MODEL_WIDTH), 1.0, 6.0, ((0, 32),)),
        "segments": jax.vmap(lambda own: jnp.searchsorted(jnp.cumsum(uneven(own, 4, LEN, LEN // 2, 0)), jnp.arange(LEN), side="right"))(jax.random.split(arg_keys[1], SEQS)).reshape((SEQS, LEN)).astype(jnp.int32),
        "gains": jnp.clip(1.0 + 0.18 * jax.random.normal(arg_keys[2], (DECODER_LAYERS, 2, MODEL_WIDTH), jnp.float32), 0.1, 1.9),
        "q_weight": draw_q_weight(jax.random.fold_in(arg_keys[11], 71), 0),
        "key_matrix": draw_key_matrix(jax.random.fold_in(arg_keys[11], 71), 0),
        "value_matrix": centred(arg_keys[5], (DECODER_LAYERS, MODEL_WIDTH, KEY_VALUE_HEADS * HEAD_SIZE), MODEL_WIDTH ** -0.5, 0.15625, ((1, 8), (2, 4))),
        "o_weight": centred(arg_keys[6], (DECODER_LAYERS, QUERY_HEADS * HEAD_SIZE, MODEL_WIDTH), (QUERY_HEADS * HEAD_SIZE // 16) ** -0.5, 0.625, ((1, 4), (2, 8))),
        "gate_weight": centred(arg_keys[7], (DECODER_LAYERS, MODEL_WIDTH, FF), MODEL_WIDTH ** -0.5, 0.15625, ((1, 8), (2, 4))),
        "up_weight": centred(arg_keys[8], (DECODER_LAYERS, MODEL_WIDTH, FF), MODEL_WIDTH ** -0.5, 0.15625, ((1, 8), (2, 4))),
        "down_weight": centred(arg_keys[9], (DECODER_LAYERS, FF, MODEL_WIDTH), FF ** -0.5, 0.09375, ((1, 4), (2, 8))),
        "cotangent": centred(arg_keys[10], (TOKENS, MODEL_WIDTH), 1.0, 6.0, ((0, 32),)),
    }


NORM_EPS = 1e-05
ROPE_BASE = 100000.0
MASKED = -1e+30

def product_mix(form, first_operand, second_operand):
    return jnp.einsum(form, first_operand.astype(jnp.float32), second_operand.astype(jnp.float32), precision=lax.Precision.HIGHEST)

def dot_last(operand, weight_full):
    return lax.dot_general(operand, weight_full, (((1,), (1,)), ((), ())), preferred_element_type=jnp.float32)

def dot_first(operand, other_operand):
    return lax.dot_general(operand, other_operand, (((0,), (0,)), ((), ())), preferred_element_type=jnp.float32)

def positions_of(segments):
    index_grid = lax.broadcasted_iota(jnp.int32, segments.shape, 1)
    starts_here = jnp.concatenate([jnp.ones((segments.shape[0], 1), jnp.bool_), segments[:, 1:] != segments[:, :-1]], axis=1)
    first_index = lax.cummax(jnp.where(starts_here, index_grid, 0), axis=1)
    return index_grid - first_index

def rope_tables(positions, head_size):
    half_size = head_size // 2
    column_index = jnp.arange(half_size).astype(jnp.float32)
    inverse_freq = jnp.exp(column_index * (-2.0 * math.log(ROPE_BASE) / head_size))
    angles = positions.astype(jnp.float32)[..., None] * inverse_freq
    return (jnp.cos(angles), jnp.sin(angles))

def rotate_halves(value_rows, cosine_table, sine_table, direction):
    half_size = value_rows.shape[-1] // 2
    first_half = value_rows[..., :half_size]
    second_half = value_rows[..., half_size:]
    cos_rows = cosine_table[:, :, None, :]
    sin_rows = direction * sine_table[:, :, None, :]
    return jnp.concatenate([first_half * cos_rows - second_half * sin_rows, second_half * cos_rows + first_half * sin_rows], axis=-1)

def score_block(block_query, seq_keys, seq_segments, block_start, block_rows):
    scores = product_mix('qhgd,khd->hgqk', block_query, seq_keys) / math.sqrt(block_query.shape[-1])
    query_index = block_start + lax.broadcasted_iota(jnp.int32, (block_rows, seq_keys.shape[0]), 0)
    key_index = lax.broadcasted_iota(jnp.int32, (block_rows, seq_keys.shape[0]), 1)
    block_segments = seq_segments[block_start:block_start + block_rows]
    allowed = (block_segments[:, None] == seq_segments[None, :]) & (key_index <= query_index)
    return jnp.where(allowed[None, None], scores, MASKED)

def attend_forward(query, key_rows, value_rows, segments):
    seq_count, length_total, query_heads, head_size = query.shape
    kv_heads = key_rows.shape[2]
    group_size = query_heads // kv_heads
    block_rows = min(512, length_total)

    def one_sequence(packed):
        seq_query, seq_keys, seq_values, seq_segments = packed
        grouped = seq_query.reshape(length_total, kv_heads, group_size, head_size)
        out_blocks = []
        lse_blocks = []
        for block_start in range(0, length_total, block_rows):
            scores = score_block(grouped[block_start:block_start + block_rows], seq_keys, seq_segments, block_start, block_rows)
            largest = lax.optimization_barrier(jnp.max(scores, axis=-1, keepdims=True))
            exp_scores = jnp.exp(scores - largest)
            row_total = lax.optimization_barrier(jnp.sum(exp_scores, axis=-1, keepdims=True))
            weights = (exp_scores / row_total).astype(jnp.bfloat16)
            out_blocks.append(product_mix('hgqk,khd->qhgd', weights, seq_values).astype(jnp.bfloat16))
            lse_blocks.append((largest + jnp.log(row_total))[..., 0])
        return (jnp.concatenate(out_blocks, 0).reshape(length_total, query_heads, head_size), jnp.concatenate(lse_blocks, -1))
    return lax.map(one_sequence, (query, key_rows, value_rows, segments))

def attend_backward(query, key_rows, value_rows, segments, attn_out, attn_lse, grad_out):
    seq_count, length_total, query_heads, head_size = query.shape
    kv_heads = key_rows.shape[2]
    group_size = query_heads // kv_heads
    block_rows = min(512, length_total)

    def one_sequence(packed):
        seq_query, seq_keys, seq_values, seq_segments, seq_out, seq_lse, seq_grad = packed
        grouped = seq_query.reshape(length_total, kv_heads, group_size, head_size)
        grouped_out = seq_out.reshape(length_total, kv_heads, group_size, head_size)
        grouped_grad = seq_grad.reshape(length_total, kv_heads, group_size, head_size)
        key_gradient = jnp.zeros((length_total, kv_heads, head_size), jnp.float32)
        value_gradient = jnp.zeros((length_total, kv_heads, head_size), jnp.float32)
        query_blocks = []
        for block_start in range(0, length_total, block_rows):
            block_end = block_start + block_rows
            block_query = grouped[block_start:block_end]
            scores = score_block(block_query, seq_keys, seq_segments, block_start, block_rows)
            probs = jnp.exp(scores - seq_lse[:, :, block_start:block_end, None])
            block_grad = grouped_grad[block_start:block_end]
            value_gradient = value_gradient + product_mix('hgqk,qhgd->khd', probs.astype(jnp.bfloat16), block_grad)
            grad_probs = product_mix('qhgd,khd->hgqk', block_grad, seq_values)
            delta = lax.optimization_barrier(jnp.sum(block_grad.astype(jnp.float32) * grouped_out[block_start:block_end].astype(jnp.float32), axis=-1))
            delta = jnp.transpose(delta, (1, 2, 0))
            grad_scores = (probs * (grad_probs - delta[..., None])).astype(jnp.bfloat16)
            query_blocks.append(product_mix('hgqk,khd->qhgd', grad_scores, seq_keys) / math.sqrt(head_size))
            key_gradient = key_gradient + product_mix('hgqk,qhgd->khd', grad_scores, block_query) / math.sqrt(head_size)
        return (jnp.concatenate(query_blocks, 0).reshape(length_total, query_heads, head_size), key_gradient, value_gradient)
    return lax.map(one_sequence, (query, key_rows, value_rows, segments, attn_out, attn_lse, grad_out))

def norm_forward(hidden_rows, gain):
    inverse_rms = lax.rsqrt(lax.optimization_barrier(jnp.mean(hidden_rows * hidden_rows, axis=-1, keepdims=True)) + NORM_EPS)
    return ((hidden_rows * inverse_rms * gain).astype(jnp.bfloat16), inverse_rms)

def norm_backward(grad_normed, hidden_rows, inverse_rms, gain, grad_rows):
    unit_rows = hidden_rows * inverse_rms
    grad_unit = grad_normed * gain
    gain_term = lax.optimization_barrier(jnp.sum(grad_normed * unit_rows, axis=0))
    new_grad = grad_rows + inverse_rms * (grad_unit - unit_rows * lax.optimization_barrier(jnp.mean(grad_unit * unit_rows, axis=-1, keepdims=True)))
    return (new_grad, gain_term)

def sequence_pass(seq_tokens, seq_segments, seq_cot, gains, q_weight, key_matrix, value_matrix, o_weight, gate_weight, up_weight, down_weight):
    length_total = seq_tokens.shape[0]
    segment_rows = seq_segments[None, :]
    cosine_table, sine_table = rope_tables(positions_of(segment_rows), HEAD_SIZE)
    residual = seq_tokens.astype(jnp.float32)
    saved = []
    for index_of_layer in range(DECODER_LAYERS):
        attention_rows, first_rms = norm_forward(residual, gains[index_of_layer, 0])
        query = rotate_halves(jnp.dot(attention_rows, q_weight[index_of_layer], preferred_element_type=jnp.float32).reshape(1, length_total, QUERY_HEADS, HEAD_SIZE), cosine_table, sine_table, 1.0).astype(jnp.bfloat16)
        key_rows = rotate_halves(jnp.dot(attention_rows, key_matrix[index_of_layer], preferred_element_type=jnp.float32).reshape(1, length_total, KEY_VALUE_HEADS, HEAD_SIZE), cosine_table, sine_table, 1.0).astype(jnp.bfloat16)
        value_rows = jnp.dot(attention_rows, value_matrix[index_of_layer], preferred_element_type=jnp.float32).astype(jnp.bfloat16).reshape(1, length_total, KEY_VALUE_HEADS, HEAD_SIZE)
        attn_out, attn_lse = attend_forward(query, key_rows, value_rows, segment_rows)
        attn_flat = attn_out.reshape(length_total, QUERY_HEADS * HEAD_SIZE)
        middle = residual + jnp.dot(attn_flat, o_weight[index_of_layer], preferred_element_type=jnp.float32)
        mlp_rows, second_rms = norm_forward(middle, gains[index_of_layer, 1])
        gate_act = jnp.dot(mlp_rows, gate_weight[index_of_layer], preferred_element_type=jnp.float32)
        up_act = jnp.dot(mlp_rows, up_weight[index_of_layer], preferred_element_type=jnp.float32)
        hidden = (jax.nn.silu(gate_act) * up_act).astype(jnp.bfloat16)
        saved.append((residual, first_rms, attention_rows, query, key_rows, value_rows, attn_out, attn_lse, attn_flat, middle, second_rms, mlp_rows, gate_act, up_act, hidden))
        residual = middle + jnp.dot(hidden, down_weight[index_of_layer], preferred_element_type=jnp.float32)
    result_rows = residual.astype(jnp.bfloat16)
    grad_rows = seq_cot.astype(jnp.float32)
    layer_grads = []
    for index_of_layer in reversed(range(DECODER_LAYERS)):
        residual_in, first_rms, attention_rows, query, key_rows, value_rows, attn_out, attn_lse, attn_flat, middle, second_rms, mlp_rows, gate_act, up_act, hidden = saved[index_of_layer]
        grad_mlp = grad_rows.astype(jnp.bfloat16)
        grad_hidden = dot_last(grad_mlp, down_weight[index_of_layer])
        down_grad = dot_first(hidden, grad_mlp)
        sigmoid_gate = jax.nn.sigmoid(gate_act)
        grad_gate = (grad_hidden * up_act * sigmoid_gate * (1.0 + gate_act * (1.0 - sigmoid_gate))).astype(jnp.bfloat16)
        grad_up = (grad_hidden * gate_act * sigmoid_gate).astype(jnp.bfloat16)
        gate_grad = dot_first(mlp_rows, grad_gate)
        up_grad = dot_first(mlp_rows, grad_up)
        grad_mlp_in = dot_last(grad_gate, gate_weight[index_of_layer])
        grad_mlp_in = grad_mlp_in + dot_last(grad_up, up_weight[index_of_layer])
        grad_rows, second_gain = norm_backward(grad_mlp_in, middle, second_rms, gains[index_of_layer, 1], grad_rows)
        grad_attn_rows = grad_rows.astype(jnp.bfloat16)
        grad_attn = dot_last(grad_attn_rows, o_weight[index_of_layer]).astype(jnp.bfloat16)
        o_grad = dot_first(attn_flat, grad_attn_rows)
        grad_query, key_gradient, value_gradient = attend_backward(query, key_rows, value_rows, segment_rows, attn_out, attn_lse, grad_attn.reshape(1, length_total, QUERY_HEADS, HEAD_SIZE))
        grad_query = rotate_halves(grad_query, cosine_table, sine_table, -1.0).astype(jnp.bfloat16).reshape(length_total, QUERY_HEADS * HEAD_SIZE)
        key_gradient = rotate_halves(key_gradient, cosine_table, sine_table, -1.0).astype(jnp.bfloat16).reshape(length_total, KEY_VALUE_HEADS * HEAD_SIZE)
        value_gradient = value_gradient.astype(jnp.bfloat16).reshape(length_total, KEY_VALUE_HEADS * HEAD_SIZE)
        q_grad = dot_first(attention_rows, grad_query)
        k_grad = dot_first(attention_rows, key_gradient)
        v_grad = dot_first(attention_rows, value_gradient)
        grad_attn_in = dot_last(grad_query, q_weight[index_of_layer])
        grad_attn_in = grad_attn_in + dot_last(key_gradient, key_matrix[index_of_layer])
        grad_attn_in = grad_attn_in + dot_last(value_gradient, value_matrix[index_of_layer])
        grad_rows, first_gain = norm_backward(grad_attn_in, residual_in, first_rms, gains[index_of_layer, 0], grad_rows)
        layer_grads.append((jnp.stack([first_gain, second_gain]), q_grad, k_grad, v_grad, o_grad, gate_grad, up_grad, down_grad))
    layer_grads = layer_grads[::-1]
    stacked = tuple((jnp.stack([grad_part[member] for grad_part in layer_grads]) for member in range(8)))
    return (result_rows, grad_rows, stacked)

def reference(tokens, segments, gains, q_weight, key_matrix, value_matrix, o_weight, gate_weight, up_weight, down_weight, cotangent):
    token_seqs = tokens.reshape(SEQS, LEN, MODEL_WIDTH)
    cot_seqs = cotangent.reshape(SEQS, LEN, MODEL_WIDTH)
    weight_list = (gains, q_weight, key_matrix, value_matrix, o_weight, gate_weight, up_weight, down_weight)
    zero_grads = tuple((jnp.zeros(weight_array.shape, jnp.float32) for weight_array in weight_list))

    def step_one(carry, packed):
        seq_tokens, seq_segments, seq_cot = packed
        result_rows, input_rows, grads = sequence_pass(seq_tokens, seq_segments, seq_cot, gains, q_weight, key_matrix, value_matrix, o_weight, gate_weight, up_weight, down_weight)
        return (tuple((carried + fresh for carried, fresh in zip(carry, grads))), (result_rows, input_rows))
    final, outputs = lax.scan(step_one, zero_grads, (token_seqs, segments, cot_seqs))
    results, input_grads = outputs
    return (results.reshape(TOKENS, MODEL_WIDTH), input_grads.reshape(TOKENS, MODEL_WIDTH), final[0], final[1], final[2], final[3], final[4], final[5], final[6], final[7])
```

```python
import math

import jax
import jax.numpy as jnp
from jax import lax
from jax.sharding import PartitionSpec as P

HEAD_SIZE = 96
DECODER_LAYERS = 2

NORM_EPS = 1e-05
ROPE_BASE = 100000.0
MASKED = -1e30


def dot_plain(operand, weight_full):
    return jnp.dot(operand, weight_full, preferred_element_type=jnp.float32)


def dot_last(operand, weight_full):
    return lax.dot_general(
        operand, weight_full, (((1,), (1,)), ((), ())), preferred_element_type=jnp.float32
    )


def dot_first(operand, other_operand):
    return lax.dot_general(
        operand, other_operand, (((0,), (0,)), ((), ())), preferred_element_type=jnp.float32
    )


def positions_of(segments):
    index_grid = lax.broadcasted_iota(jnp.int32, segments.shape, 1)
    starts_here = jnp.concatenate(
        [jnp.ones((segments.shape[0], 1), jnp.bool_), segments[:, 1:] != segments[:, :-1]], axis=1
    )
    first_index = lax.cummax(jnp.where(starts_here, index_grid, 0), axis=1)
    return index_grid - first_index


def rope_tables(positions, head_size):
    half_size = head_size // 2
    column_index = jnp.arange(half_size).astype(jnp.float32)
    inverse_freq = jnp.exp(column_index * (-2.0 * math.log(ROPE_BASE) / head_size))
    angles = positions.astype(jnp.float32)[..., None] * inverse_freq
    return (jnp.cos(angles), jnp.sin(angles))


def rotate_halves(value_rows, cosine_table, sine_table, direction):
    half_size = value_rows.shape[-1] // 2
    first_half = value_rows[..., :half_size]
    second_half = value_rows[..., half_size:]
    cos_rows = cosine_table[:, None, :]
    sin_rows = direction * sine_table[:, None, :]
    return jnp.concatenate(
        [
            first_half * cos_rows - second_half * sin_rows,
            second_half * cos_rows + first_half * sin_rows,
        ],
        axis=-1,
    )


def swap(rows, offset):
    size = lax.axis_size("tensor")
    return lax.ppermute(rows, "tensor", [(i, i ^ offset) for i in range(size)])


def gather_rows(rows):
    size = lax.axis_size("tensor")
    if size != 4:
        return [rows] + [swap(rows, offset) for offset in range(1, size)]
    half = rows.shape[0] // 2
    near = swap(rows, 1)
    far = swap(rows, 2)
    cross = jnp.concatenate([swap(near[:half], 2), swap(far[half:], 1)], axis=0)
    return [rows, near, far, cross]


def scatter_sum(partials):
    size = lax.axis_size("tensor")
    sent = jnp.bfloat16
    if size != 4:
        total = partials[0]
        for offset in range(1, size):
            total = total + swap(partials[offset].astype(sent), offset).astype(jnp.float32)
        return total
    own, near, far, cross = partials
    half = own.shape[0] // 2
    cross = cross.astype(sent)
    upper = swap(cross[:half], 1).astype(jnp.float32)
    lower = swap(cross[half:], 2).astype(jnp.float32)
    near = jnp.concatenate([near[:half], near[half:] + lower], axis=0).astype(sent)
    far = jnp.concatenate([far[:half] + upper, far[half:]], axis=0).astype(sent)
    return own + swap(near, 1).astype(jnp.float32) + swap(far, 2).astype(jnp.float32)


def gather_weights(shard):
    return lax.all_gather(shard, "dp", axis=0, tiled=True)


def scatter_grads(partial):
    return lax.psum_scatter(
        partial.astype(jnp.bfloat16), "dp", scatter_dimension=0, tiled=True
    ).astype(jnp.float32)


def score_rows(grouped, key_rows, allowed):
    scores = jnp.einsum(
        "qhgd,khd->hgqk", grouped, key_rows, preferred_element_type=jnp.float32
    ) / math.sqrt(HEAD_SIZE)
    return jnp.where(allowed[None, None], scores, MASKED)


def attend_forward(query, key_rows, value_rows, allowed):
    length_total, query_heads, head_size = query.shape
    kv_heads = key_rows.shape[1]
    grouped = query.reshape(length_total, kv_heads, query_heads // kv_heads, head_size)
    scores = score_rows(grouped, key_rows, allowed)
    largest = jnp.max(scores, axis=-1, keepdims=True)
    exp_scores = jnp.exp(scores - largest)
    row_total = jnp.sum(exp_scores, axis=-1, keepdims=True)
    weights = (exp_scores / row_total).astype(jnp.bfloat16)
    out = jnp.einsum(
        "hgqk,khd->qhgd", weights, value_rows, preferred_element_type=jnp.float32
    ).astype(jnp.bfloat16)
    return (
        out.reshape(length_total, query_heads, head_size),
        (largest + jnp.log(row_total))[..., 0],
    )


def attend_backward(query, key_rows, value_rows, allowed, attn_out, attn_lse, grad_out):
    length_total, query_heads, head_size = query.shape
    kv_heads = key_rows.shape[1]
    grouped_shape = (length_total, kv_heads, query_heads // kv_heads, head_size)
    grouped = query.reshape(grouped_shape)
    grouped_out = attn_out.reshape(grouped_shape)
    grouped_grad = grad_out.reshape(grouped_shape)
    scores = score_rows(grouped, key_rows, allowed)
    probs = jnp.exp(scores - attn_lse[..., None])
    value_gradient = jnp.einsum(
        "hgqk,qhgd->khd",
        probs.astype(jnp.bfloat16),
        grouped_grad,
        preferred_element_type=jnp.float32,
    )
    grad_probs = jnp.einsum(
        "qhgd,khd->hgqk", grouped_grad, value_rows, preferred_element_type=jnp.float32
    )
    delta = jnp.sum(grouped_grad.astype(jnp.float32) * grouped_out.astype(jnp.float32), axis=-1)
    delta = jnp.transpose(delta, (1, 2, 0))
    grad_scores = (probs * (grad_probs - delta[..., None])).astype(jnp.bfloat16)
    query_gradient = jnp.einsum(
        "hgqk,khd->qhgd", grad_scores, key_rows, preferred_element_type=jnp.float32
    ) / math.sqrt(head_size)
    key_gradient = jnp.einsum(
        "hgqk,qhgd->khd", grad_scores, grouped, preferred_element_type=jnp.float32
    ) / math.sqrt(head_size)
    return query_gradient.reshape(query.shape), key_gradient, value_gradient


def norm_forward(hidden_rows, gain):
    inverse_rms = lax.rsqrt(jnp.mean(hidden_rows * hidden_rows, axis=-1, keepdims=True) + NORM_EPS)
    return ((hidden_rows * inverse_rms * gain).astype(jnp.bfloat16), inverse_rms)


def norm_backward(grad_normed, hidden_rows, inverse_rms, gain, grad_rows):
    unit_rows = hidden_rows * inverse_rms
    grad_unit = grad_normed * gain
    gain_term = jnp.sum(grad_normed * unit_rows, axis=0)
    new_grad = grad_rows + inverse_rms * (
        grad_unit - unit_rows * jnp.mean(grad_unit * unit_rows, axis=-1, keepdims=True)
    )
    return (new_grad, gain_term)


def body(
    tokens,
    segments,
    gains,
    q_weight,
    key_matrix,
    value_matrix,
    o_weight,
    gate_weight,
    up_weight,
    down_weight,
    cotangent,
):
    tensor_size = lax.axis_size("tensor")
    local_rows = tokens.shape[0]
    q_cols = q_weight.shape[2]
    kv_cols = key_matrix.shape[2]
    ff_cols = gate_weight.shape[2]
    query_heads = q_cols // HEAD_SIZE
    kv_heads = kv_cols // HEAD_SIZE
    length_total = segments.shape[1]

    weights = []
    for layer in range(DECODER_LAYERS):
        qkv = gather_weights(
            jnp.concatenate([q_weight[layer], key_matrix[layer], value_matrix[layer]], axis=1)
        )
        out = gather_weights(o_weight[layer].T)
        gate_up = gather_weights(jnp.concatenate([gate_weight[layer], up_weight[layer]], axis=1))
        down = gather_weights(down_weight[layer].T)
        weights.append((qkv, out, gate_up, down))

    me = lax.axis_index("tensor")
    block_at = me ^ jnp.arange(tensor_size, dtype=jnp.int32)
    order = (
        block_at[:, None] * local_rows + jnp.arange(local_rows, dtype=jnp.int32)[None]
    ).reshape(-1)
    positions = positions_of(segments)[0]

    def reorder(values):
        return jnp.concatenate(
            [
                lax.dynamic_slice_in_dim(values, block_at[k] * local_rows, local_rows, 0)
                for k in range(tensor_size)
            ],
            axis=0,
        )

    segment_ids = reorder(segments[0])
    cosine_table, sine_table = rope_tables(reorder(positions), HEAD_SIZE)
    allowed = (segment_ids[:, None] == segment_ids[None, :]) & (order[None, :] <= order[:, None])

    def blocks_of(values):
        return [values[k * local_rows : (k + 1) * local_rows] for k in range(tensor_size)]

    residual = tokens.astype(jnp.float32)
    saved = []
    for layer in range(DECODER_LAYERS):
        qkv_full, out_full, gate_up_full, down_full = weights[layer]
        normed, first_rms = norm_forward(residual, gains[layer, 0])
        attn_blocks = gather_rows(normed)
        projected = jnp.concatenate([dot_plain(rows, qkv_full) for rows in attn_blocks], axis=0)
        query = rotate_halves(
            projected[:, :q_cols].reshape(length_total, query_heads, HEAD_SIZE),
            cosine_table,
            sine_table,
            1.0,
        ).astype(jnp.bfloat16)
        key_rows = rotate_halves(
            projected[:, q_cols : q_cols + kv_cols].reshape(length_total, kv_heads, HEAD_SIZE),
            cosine_table,
            sine_table,
            1.0,
        ).astype(jnp.bfloat16)
        value_rows = (
            projected[:, q_cols + kv_cols :]
            .astype(jnp.bfloat16)
            .reshape(length_total, kv_heads, HEAD_SIZE)
        )
        attn_out, attn_lse = attend_forward(query, key_rows, value_rows, allowed)
        attn_flat = attn_out.reshape(length_total, q_cols)
        middle = residual + scatter_sum([dot_last(rows, out_full) for rows in blocks_of(attn_flat)])
        normed2, second_rms = norm_forward(middle, gains[layer, 1])
        mlp_blocks = gather_rows(normed2)
        gate_blocks = []
        up_blocks = []
        hidden_blocks = []
        for rows in mlp_blocks:
            gate_act = dot_plain(rows, gate_up_full[:, :ff_cols])
            up_act = dot_plain(rows, gate_up_full[:, ff_cols:])
            gate_blocks.append(gate_act)
            up_blocks.append(up_act)
            hidden_blocks.append((jax.nn.silu(gate_act) * up_act).astype(jnp.bfloat16))
        saved.append(
            (
                residual,
                first_rms,
                attn_blocks,
                query,
                key_rows,
                value_rows,
                attn_out,
                attn_lse,
                attn_flat,
                middle,
                second_rms,
                mlp_blocks,
                gate_blocks,
                up_blocks,
                hidden_blocks,
            )
        )
        residual = middle + scatter_sum([dot_last(rows, down_full) for rows in hidden_blocks])
    result = residual.astype(jnp.bfloat16)

    grad_rows = cotangent.astype(jnp.float32)
    gain_terms = [None] * DECODER_LAYERS
    weight_grads = [None] * DECODER_LAYERS
    for layer in reversed(range(DECODER_LAYERS)):
        (
            residual_in,
            first_rms,
            attn_blocks,
            query,
            key_rows,
            value_rows,
            attn_out,
            attn_lse,
            attn_flat,
            middle,
            second_rms,
            mlp_blocks,
            gate_blocks,
            up_blocks,
            hidden_blocks,
        ) = saved[layer]
        qkv_full, out_full, gate_up_full, down_full = weights[layer]
        grad_mlp_blocks = gather_rows(grad_rows.astype(jnp.bfloat16))
        grad_gate_up_blocks = []
        partials = []
        for k in range(tensor_size):
            grad_hidden = dot_plain(grad_mlp_blocks[k], down_full)
            gate_act = gate_blocks[k]
            up_act = up_blocks[k]
            sigmoid_gate = jax.nn.sigmoid(gate_act)
            grad_gate = (
                grad_hidden * up_act * sigmoid_gate * (1.0 + gate_act * (1.0 - sigmoid_gate))
            ).astype(jnp.bfloat16)
            grad_up = (grad_hidden * gate_act * sigmoid_gate).astype(jnp.bfloat16)
            grad_gate_up = jnp.concatenate([grad_gate, grad_up], axis=1)
            grad_gate_up_blocks.append(grad_gate_up)
            partials.append(dot_last(grad_gate_up, gate_up_full))
        grad_mlp_in = scatter_sum(partials)
        down_grad = dot_first(
            jnp.concatenate(grad_mlp_blocks, axis=0), jnp.concatenate(hidden_blocks, axis=0)
        )
        gate_up_grad = dot_first(
            jnp.concatenate(mlp_blocks, axis=0), jnp.concatenate(grad_gate_up_blocks, axis=0)
        )
        gate_up_grad = scatter_grads(gate_up_grad)
        down_grad = scatter_grads(down_grad)
        grad_rows, second_gain = norm_backward(
            grad_mlp_in, middle, second_rms, gains[layer, 1], grad_rows
        )
        grad_attn_blocks = gather_rows(grad_rows.astype(jnp.bfloat16))
        grad_attn = jnp.concatenate(
            [dot_plain(rows, out_full).astype(jnp.bfloat16) for rows in grad_attn_blocks], axis=0
        )
        out_grad = dot_first(jnp.concatenate(grad_attn_blocks, axis=0), attn_flat)
        out_grad = scatter_grads(out_grad)
        grad_query, key_gradient, value_gradient = attend_backward(
            query,
            key_rows,
            value_rows,
            allowed,
            attn_out,
            attn_lse,
            grad_attn.reshape(length_total, query_heads, HEAD_SIZE),
        )
        grad_query = rotate_halves(grad_query, cosine_table, sine_table, -1.0)
        key_gradient = rotate_halves(key_gradient, cosine_table, sine_table, -1.0)
        grad_qkv = jnp.concatenate(
            [
                grad_query.astype(jnp.bfloat16).reshape(length_total, q_cols),
                key_gradient.astype(jnp.bfloat16).reshape(length_total, kv_cols),
                value_gradient.astype(jnp.bfloat16).reshape(length_total, kv_cols),
            ],
            axis=1,
        )
        grad_attn_in = scatter_sum([dot_last(rows, qkv_full) for rows in blocks_of(grad_qkv)])
        qkv_grad = dot_first(jnp.concatenate(attn_blocks, axis=0), grad_qkv)
        qkv_grad = scatter_grads(qkv_grad)
        grad_rows, first_gain = norm_backward(
            grad_attn_in, residual_in, first_rms, gains[layer, 0], grad_rows
        )
        weight_grads[layer] = (
            qkv_grad[:, :q_cols],
            qkv_grad[:, q_cols : q_cols + kv_cols],
            qkv_grad[:, q_cols + kv_cols :],
            out_grad.T,
            gate_up_grad[:, :ff_cols],
            gate_up_grad[:, ff_cols:],
            down_grad.T,
        )
        gain_terms[layer] = jnp.stack([first_gain, second_gain])
    gains_grad = lax.psum_scatter(
        jnp.stack(gain_terms), ("dp", "tensor"), scatter_dimension=2, tiled=True
    )
    stacked = [jnp.stack([parts[member] for parts in weight_grads]) for member in range(7)]
    return (result, grad_rows, gains_grad, *stacked)


def solution(mesh):
    in_specs = (
        P(("dp", "tensor"), None),
        P("dp", None),
        P(),
        P(None, "dp", "tensor"),
        P(None, "dp", "tensor"),
        P(None, "dp", "tensor"),
        P(None, "tensor", "dp"),
        P(None, "dp", "tensor"),
        P(None, "dp", "tensor"),
        P(None, "tensor", "dp"),
        P(("dp", "tensor"), None),
    )
    out_specs = (
        P(("dp", "tensor"), None),
        P(("dp", "tensor"), None),
        P(None, None, ("dp", "tensor")),
        P(None, "dp", "tensor"),
        P(None, "dp", "tensor"),
        P(None, "dp", "tensor"),
        P(None, "tensor", "dp"),
        P(None, "dp", "tensor"),
        P(None, "dp", "tensor"),
        P(None, "tensor", "dp"),
    )
    return jax.shard_map(body, mesh=mesh, in_specs=in_specs, out_specs=out_specs, check_vma=False)
```

```python
import functools
import math

import jax
import jax.numpy as jnp
from jax import lax
from jax.experimental import pallas as pl
from jax.experimental.pallas import tpu as pltpu
from jax.sharding import PartitionSpec as P

HEAD_SIZE = 96
DECODER_LAYERS = 2

NORM_EPS = 1e-05
ROPE_BASE = 100000.0
MASKED = -1e30


def dot_plain(operand, weight_full):
    return jnp.dot(operand, weight_full, preferred_element_type=jnp.float32)


def dot_last(operand, weight_full):
    return lax.dot_general(
        operand, weight_full, (((1,), (1,)), ((), ())), preferred_element_type=jnp.float32
    )


def dot_first(operand, other_operand):
    return lax.dot_general(
        operand, other_operand, (((0,), (0,)), ((), ())), preferred_element_type=jnp.float32
    )


def positions_of(segments):
    index_grid = lax.broadcasted_iota(jnp.int32, segments.shape, 1)
    starts_here = jnp.concatenate(
        [jnp.ones((segments.shape[0], 1), jnp.bool_), segments[:, 1:] != segments[:, :-1]], axis=1
    )
    first_index = lax.cummax(jnp.where(starts_here, index_grid, 0), axis=1)
    return index_grid - first_index


def rope_tables(positions, head_size):
    half_size = head_size // 2
    column_index = jnp.arange(half_size).astype(jnp.float32)
    inverse_freq = jnp.exp(column_index * (-2.0 * math.log(ROPE_BASE) / head_size))
    angles = positions.astype(jnp.float32)[..., None] * inverse_freq
    return (jnp.cos(angles), jnp.sin(angles))


def rotate_halves(value_rows, cosine_table, sine_table, direction):
    half_size = value_rows.shape[-1] // 2
    first_half = value_rows[..., :half_size]
    second_half = value_rows[..., half_size:]
    cos_rows = cosine_table[:, None, :]
    sin_rows = direction * sine_table[:, None, :]
    return jnp.concatenate(
        [
            first_half * cos_rows - second_half * sin_rows,
            second_half * cos_rows + first_half * sin_rows,
        ],
        axis=-1,
    )


def swap(rows, offset):
    size = lax.axis_size("tensor")
    return lax.ppermute(rows, "tensor", [(i, i ^ offset) for i in range(size)])


def gather_rows(rows):
    size = lax.axis_size("tensor")
    if size != 4:
        return [rows] + [swap(rows, offset) for offset in range(1, size)]
    half = rows.shape[0] // 2
    near = swap(rows, 1)
    far = swap(rows, 2)
    cross = jnp.concatenate([swap(near[:half], 2), swap(far[half:], 1)], axis=0)
    return [rows, near, far, cross]


def scatter_sum(partials):
    size = lax.axis_size("tensor")
    sent = jnp.bfloat16
    if size != 4:
        total = partials[0]
        for offset in range(1, size):
            total = total + swap(partials[offset].astype(sent), offset).astype(jnp.float32)
        return total
    own, near, far, cross = partials
    half = own.shape[0] // 2
    cross = cross.astype(sent)
    upper = swap(cross[:half], 1).astype(jnp.float32)
    lower = swap(cross[half:], 2).astype(jnp.float32)
    near = jnp.concatenate([near[:half], near[half:] + lower], axis=0).astype(sent)
    far = jnp.concatenate([far[:half] + upper, far[half:]], axis=0).astype(sent)
    return own + swap(near, 1).astype(jnp.float32) + swap(far, 2).astype(jnp.float32)


def gather_weights(shard):
    return lax.all_gather(shard, "dp", axis=0, tiled=True)


def scatter_grads(partial):
    return lax.psum_scatter(partial, "dp", scatter_dimension=0, tiled=True).astype(jnp.float32)


def weight_grad_kernel(pair_sizes, *refs):
    out_ref = refs[-1]
    at = 0
    column = 0
    for size in pair_sizes:
        width = refs[at + size].shape[1]
        total = None
        for k in range(size):
            term = dot_first(refs[at + k][...], refs[at + size + k][...])
            total = term if total is None else total + term
        out_ref[:, column : column + width] = total.astype(out_ref.dtype)
        at += 2 * size
        column += width


def weight_grads_of(pairs):
    rows = pairs[0][0][0].shape[0]
    depth = pairs[0][0][0].shape[1]
    tile = 256
    operands = []
    in_specs = []
    columns = 0
    for inputs, grads in pairs:
        operands += list(inputs) + list(grads)
        in_specs += [pl.BlockSpec((rows, tile), lambda i: (0, i))] * len(inputs)
        in_specs += [pl.BlockSpec(grad.shape, lambda i: (0, 0)) for grad in grads]
        columns += grads[0].shape[1]
    total_rows = rows * len(pairs[0][0])
    return pl.pallas_call(
        functools.partial(weight_grad_kernel, tuple(len(inputs) for inputs, _ in pairs)),
        grid=(depth // tile,),
        in_specs=in_specs,
        out_specs=pl.BlockSpec((tile, columns), lambda i: (i, 0)),
        out_shape=jax.ShapeDtypeStruct((depth, columns), jnp.bfloat16),
        compiler_params=pltpu.CompilerParams(vmem_limit_bytes=40 << 20),
        cost_estimate=pl.CostEstimate(
            flops=2 * total_rows * depth * columns,
            bytes_accessed=2 * (total_rows * (depth + columns) + depth * columns),
            transcendentals=0,
        ),
        name="weight_grads",
    )(*operands)


def tie(value, other):
    return lax.optimization_barrier((value, other))


def scatter_gains(terms):
    axes = ("dp", "tensor")
    count = lax.axis_size("dp") * lax.axis_size("tensor")
    me = lax.axis_index("dp") * lax.axis_size("tensor") + lax.axis_index("tensor")
    layers, sides, width = terms.shape
    parts = terms.reshape(layers * sides, count, width // count).transpose(1, 0, 2)
    step = count // 2
    while step:
        upper = (me // step) % 2
        kept = lax.dynamic_slice_in_dim(parts, upper * step, step, 0)
        sent = lax.dynamic_slice_in_dim(parts, (1 - upper) * step, step, 0)
        parts = kept + lax.ppermute(sent, axes, [(i, i ^ step) for i in range(count)])
        step //= 2
    return parts.reshape(layers, sides, width // count)


def score_rows(grouped, key_rows, allowed):
    scores = jnp.einsum(
        "qhgd,khd->hgqk", grouped, key_rows, preferred_element_type=jnp.float32
    ) / math.sqrt(HEAD_SIZE)
    return jnp.where(allowed[None, None], scores, MASKED)


def attend_forward(query, key_rows, value_rows, allowed):
    length_total, query_heads, head_size = query.shape
    kv_heads = key_rows.shape[1]
    grouped = query.reshape(length_total, kv_heads, query_heads // kv_heads, head_size)
    scores = score_rows(grouped, key_rows, allowed)
    largest = jnp.max(scores, axis=-1, keepdims=True)
    exp_scores = jnp.exp(scores - largest)
    row_total = jnp.sum(exp_scores, axis=-1, keepdims=True)
    weights = (exp_scores / row_total).astype(jnp.bfloat16)
    out = jnp.einsum(
        "hgqk,khd->qhgd", weights, value_rows, preferred_element_type=jnp.float32
    ).astype(jnp.bfloat16)
    return (
        out.reshape(length_total, query_heads, head_size),
        (largest + jnp.log(row_total))[..., 0],
    )


def attend_backward(query, key_rows, value_rows, allowed, attn_out, attn_lse, grad_out):
    length_total, query_heads, head_size = query.shape
    kv_heads = key_rows.shape[1]
    grouped_shape = (length_total, kv_heads, query_heads // kv_heads, head_size)
    grouped = query.reshape(grouped_shape)
    grouped_out = attn_out.reshape(grouped_shape)
    grouped_grad = grad_out.reshape(grouped_shape)
    scores = score_rows(grouped, key_rows, allowed)
    probs = jnp.exp(scores - attn_lse[..., None])
    value_gradient = jnp.einsum(
        "hgqk,qhgd->khd",
        probs.astype(jnp.bfloat16),
        grouped_grad,
        preferred_element_type=jnp.float32,
    )
    grad_probs = jnp.einsum(
        "qhgd,khd->hgqk", grouped_grad, value_rows, preferred_element_type=jnp.float32
    )
    delta = jnp.sum(grouped_grad.astype(jnp.float32) * grouped_out.astype(jnp.float32), axis=-1)
    delta = jnp.transpose(delta, (1, 2, 0))
    grad_scores = (probs * (grad_probs - delta[..., None])).astype(jnp.bfloat16)
    query_gradient = jnp.einsum(
        "hgqk,khd->qhgd", grad_scores, key_rows, preferred_element_type=jnp.float32
    ) / math.sqrt(head_size)
    key_gradient = jnp.einsum(
        "hgqk,qhgd->khd", grad_scores, grouped, preferred_element_type=jnp.float32
    ) / math.sqrt(head_size)
    return query_gradient.reshape(query.shape), key_gradient, value_gradient


def norm_forward(hidden_rows, gain):
    inverse_rms = lax.rsqrt(jnp.mean(hidden_rows * hidden_rows, axis=-1, keepdims=True) + NORM_EPS)
    return ((hidden_rows * inverse_rms * gain).astype(jnp.bfloat16), inverse_rms)


def norm_backward(grad_normed, hidden_rows, inverse_rms, gain, grad_rows):
    unit_rows = hidden_rows * inverse_rms
    grad_unit = grad_normed * gain
    gain_term = jnp.sum(grad_normed * unit_rows, axis=0)
    new_grad = grad_rows + inverse_rms * (
        grad_unit - unit_rows * jnp.mean(grad_unit * unit_rows, axis=-1, keepdims=True)
    )
    return (new_grad, gain_term)


def body(
    tokens,
    segments,
    gains,
    q_weight,
    key_matrix,
    value_matrix,
    o_weight,
    gate_weight,
    up_weight,
    down_weight,
    cotangent,
):
    tensor_size = lax.axis_size("tensor")
    local_rows = tokens.shape[0]
    q_cols = q_weight.shape[2]
    kv_cols = key_matrix.shape[2]
    ff_cols = gate_weight.shape[2]
    query_heads = q_cols // HEAD_SIZE
    kv_heads = kv_cols // HEAD_SIZE
    length_total = segments.shape[1]

    weights = []
    for layer in range(DECODER_LAYERS):
        qkv = gather_weights(
            jnp.concatenate([q_weight[layer], key_matrix[layer], value_matrix[layer]], axis=1)
        )
        out = gather_weights(o_weight[layer].T)
        gate_up = gather_weights(jnp.concatenate([gate_weight[layer], up_weight[layer]], axis=1))
        down = gather_weights(down_weight[layer].T)
        weights.append((qkv, out, gate_up, down))

    me = lax.axis_index("tensor")
    block_at = me ^ jnp.arange(tensor_size, dtype=jnp.int32)
    order = (
        block_at[:, None] * local_rows + jnp.arange(local_rows, dtype=jnp.int32)[None]
    ).reshape(-1)
    positions = positions_of(segments)[0]

    def reorder(values):
        return jnp.concatenate(
            [
                lax.dynamic_slice_in_dim(values, block_at[k] * local_rows, local_rows, 0)
                for k in range(tensor_size)
            ],
            axis=0,
        )

    segment_ids = reorder(segments[0])
    cosine_table, sine_table = rope_tables(reorder(positions), HEAD_SIZE)
    allowed = (segment_ids[:, None] == segment_ids[None, :]) & (order[None, :] <= order[:, None])

    def blocks_of(values):
        return [values[k * local_rows : (k + 1) * local_rows] for k in range(tensor_size)]

    residual = tokens.astype(jnp.float32)
    saved = []
    for layer in range(DECODER_LAYERS):
        qkv_full, out_full, gate_up_full, down_full = weights[layer]
        normed, first_rms = norm_forward(residual, gains[layer, 0])
        attn_blocks = gather_rows(normed)
        projected = jnp.concatenate([dot_plain(rows, qkv_full) for rows in attn_blocks], axis=0)
        query = rotate_halves(
            projected[:, :q_cols].reshape(length_total, query_heads, HEAD_SIZE),
            cosine_table,
            sine_table,
            1.0,
        ).astype(jnp.bfloat16)
        key_rows = rotate_halves(
            projected[:, q_cols : q_cols + kv_cols].reshape(length_total, kv_heads, HEAD_SIZE),
            cosine_table,
            sine_table,
            1.0,
        ).astype(jnp.bfloat16)
        value_rows = (
            projected[:, q_cols + kv_cols :]
            .astype(jnp.bfloat16)
            .reshape(length_total, kv_heads, HEAD_SIZE)
        )
        attn_out, attn_lse = attend_forward(query, key_rows, value_rows, allowed)
        attn_flat = attn_out.reshape(length_total, q_cols)
        middle = residual + scatter_sum([dot_last(rows, out_full) for rows in blocks_of(attn_flat)])
        normed2, second_rms = norm_forward(middle, gains[layer, 1])
        mlp_blocks = gather_rows(normed2)
        gate_blocks = []
        up_blocks = []
        hidden_blocks = []
        for rows in mlp_blocks:
            gate_act = dot_plain(rows, gate_up_full[:, :ff_cols])
            up_act = dot_plain(rows, gate_up_full[:, ff_cols:])
            gate_blocks.append(gate_act)
            up_blocks.append(up_act)
            hidden_blocks.append((jax.nn.silu(gate_act) * up_act).astype(jnp.bfloat16))
        saved.append(
            (
                residual,
                first_rms,
                attn_blocks,
                query,
                key_rows,
                value_rows,
                attn_out,
                attn_lse,
                attn_flat,
                middle,
                second_rms,
                mlp_blocks,
                gate_blocks,
                up_blocks,
                hidden_blocks,
            )
        )
        residual = middle + scatter_sum([dot_last(rows, down_full) for rows in hidden_blocks])
    result = residual.astype(jnp.bfloat16)

    grad_rows = cotangent.astype(jnp.float32)
    gain_terms = [None] * DECODER_LAYERS
    weight_grads = [None] * DECODER_LAYERS
    for layer in reversed(range(DECODER_LAYERS)):
        (
            residual_in,
            first_rms,
            attn_blocks,
            query,
            key_rows,
            value_rows,
            attn_out,
            attn_lse,
            attn_flat,
            middle,
            second_rms,
            mlp_blocks,
            gate_blocks,
            up_blocks,
            hidden_blocks,
        ) = saved[layer]
        qkv_full, out_full, gate_up_full, down_full = weights[layer]
        grad_mlp_blocks = gather_rows(grad_rows.astype(jnp.bfloat16))
        grad_gate_up_blocks = []
        partials = []
        for k in range(tensor_size):
            grad_hidden = dot_plain(grad_mlp_blocks[k], down_full)
            gate_act = gate_blocks[k]
            up_act = up_blocks[k]
            sigmoid_gate = jax.nn.sigmoid(gate_act)
            grad_gate = (
                grad_hidden * up_act * sigmoid_gate * (1.0 + gate_act * (1.0 - sigmoid_gate))
            ).astype(jnp.bfloat16)
            grad_up = (grad_hidden * gate_act * sigmoid_gate).astype(jnp.bfloat16)
            grad_gate_up = jnp.concatenate([grad_gate, grad_up], axis=1)
            grad_gate_up_blocks.append(grad_gate_up)
            partials.append(dot_last(grad_gate_up, gate_up_full))
        grad_mlp_in = scatter_sum(partials)
        mlp_grad = weight_grads_of(
            [(mlp_blocks, grad_gate_up_blocks), (grad_mlp_blocks, hidden_blocks)]
        )
        grad_rows, second_gain = norm_backward(
            grad_mlp_in, middle, second_rms, gains[layer, 1], grad_rows
        )
        grad_rows, mlp_grad = tie(grad_rows, mlp_grad)
        mlp_grad = scatter_grads(mlp_grad)
        grad_attn_blocks = gather_rows(grad_rows.astype(jnp.bfloat16))
        grad_attn = jnp.concatenate(
            [dot_plain(rows, out_full).astype(jnp.bfloat16) for rows in grad_attn_blocks], axis=0
        )
        grad_query, key_gradient, value_gradient = attend_backward(
            query,
            key_rows,
            value_rows,
            allowed,
            attn_out,
            attn_lse,
            grad_attn.reshape(length_total, query_heads, HEAD_SIZE),
        )
        grad_query = rotate_halves(grad_query, cosine_table, sine_table, -1.0)
        key_gradient = rotate_halves(key_gradient, cosine_table, sine_table, -1.0)
        grad_qkv = jnp.concatenate(
            [
                grad_query.astype(jnp.bfloat16).reshape(length_total, q_cols),
                key_gradient.astype(jnp.bfloat16).reshape(length_total, kv_cols),
                value_gradient.astype(jnp.bfloat16).reshape(length_total, kv_cols),
            ],
            axis=1,
        )
        grad_attn_in = scatter_sum([dot_last(rows, qkv_full) for rows in blocks_of(grad_qkv)])
        attn_grad = weight_grads_of(
            [(attn_blocks, blocks_of(grad_qkv)), (grad_attn_blocks, blocks_of(attn_flat))]
        )
        grad_rows, first_gain = norm_backward(
            grad_attn_in, residual_in, first_rms, gains[layer, 0], grad_rows
        )
        if layer:
            grad_rows, attn_grad = tie(grad_rows, attn_grad)
        attn_grad = scatter_grads(attn_grad)
        weight_grads[layer] = (
            attn_grad[:, :q_cols],
            attn_grad[:, q_cols : q_cols + kv_cols],
            attn_grad[:, q_cols + kv_cols : q_cols + 2 * kv_cols],
            attn_grad[:, q_cols + 2 * kv_cols :].T,
            mlp_grad[:, :ff_cols],
            mlp_grad[:, ff_cols : 2 * ff_cols],
            mlp_grad[:, 2 * ff_cols :].T,
        )
        gain_terms[layer] = jnp.stack([first_gain, second_gain])
    gains_grad = scatter_gains(jnp.stack(gain_terms))
    stacked = [jnp.stack([parts[member] for parts in weight_grads]) for member in range(7)]
    return (result, grad_rows, gains_grad, *stacked)


def solution(mesh):
    in_specs = (
        P(("dp", "tensor"), None),
        P("dp", None),
        P(),
        P(None, "dp", "tensor"),
        P(None, "dp", "tensor"),
        P(None, "dp", "tensor"),
        P(None, "tensor", "dp"),
        P(None, "dp", "tensor"),
        P(None, "dp", "tensor"),
        P(None, "tensor", "dp"),
        P(("dp", "tensor"), None),
    )
    out_specs = (
        P(("dp", "tensor"), None),
        P(("dp", "tensor"), None),
        P(None, None, ("dp", "tensor")),
        P(None, "dp", "tensor"),
        P(None, "dp", "tensor"),
        P(None, "dp", "tensor"),
        P(None, "tensor", "dp"),
        P(None, "dp", "tensor"),
        P(None, "dp", "tensor"),
        P(None, "tensor", "dp"),
    )
    return jax.shard_map(body, mesh=mesh, in_specs=in_specs, out_specs=out_specs, check_vma=False)
```
